256 devices in a mesh: req: 32 (over x, z), tp: 8 (over y, core).
Axes of the slice: x: 4, y: 4, z: 8, core: 2. Of those that a mesh axis runs over, the one named last changes fastest.
Arguments:
- inputs: bfloat16 [128, 1280], P('req'), may hold values from -6 to 6
- gain_attn: float32 [1280], replicated, may hold values from 0.25 to 1.75
- w_qkv: bfloat16 [3, 1280, 1280], P(None, 'tp'), may hold values from -0.15625 to 0.15625
- k_cache: bfloat16 [128, 1280, 2048], P('req', 'tp'), may hold values from -800 to 800
- v_cache: bfloat16 [128, 1280, 2048], P('req', 'tp'), may hold values from -6 to 6
- lengths: int32 [128], P('req'), may hold values from 128 to 2048, as said below
- pad_mask: int32 [128, 2048], P('req'), may hold values 0 or 1
- w_out: bfloat16 [1280, 1280], P('tp'), may hold values from -0.15625 to 0.15625
- gain_mlp: float32 [1280], replicated, may hold values from 0.25 to 1.75
- w_up: bfloat16 [1280, 1280], P('tp'), may hold values from -0.15625 to 0.15625
- w_down: bfloat16 [1280, 1280], P('tp'), may hold values from -0.15625 to 0.15625
- w_head: bfloat16 [1280, 1280], P('tp'), may hold values from -0.15625 to 0.15625
- placement: int32 [2, 64], replicated, may hold values from 0 to 63, as said below
- guide: float32 [64], P('req'), may hold values from 1.5 to 6
Outputs:
- guided: float32 [64, 1280], P('req', 'tp')
The draws below stay inside these ranges and needn't reach their ends.
Inputs may be any that keep to these rules, and one draw needn't show every extreme that they name: `lengths`: some request has exactly 2048 filled slots. `placement`: each of the two rows is a permutation of 0 to 63.
All inputs are finite; a program needn't handle non-finite values. No bound on the sum of `pad_mask` on one device may be relied on, other than what follows from the above.
Results may differ from the reference program's by a relative error of at most 0.0085.
Values may be sent and summed in bfloat16 or wider, within the bound.
No kernel may reach another device: no remote copies, remote signals or barrier semaphores. Data moves between devices by JAX's collectives and lax.ppermute only.
A program may use at most 64 MiB of HBM per device.

```python
import math
import jax
import jax.numpy as jnp
from jax import lax

D = 1280
HEADS = 16
HEAD_DIM = 80
FF = 1280
OUT = 1280
CTX = 2048
PAIRS = 64
ROWS = 128


def draw_k_cache(key, part):
    shape = (ROWS, HEADS * HEAD_DIM, CTX)
    return jnp.clip(jax.random.normal(key, shape, jnp.float32), -6.0, 6.0).astype(jnp.bfloat16)


def draw_lengths(key, part):
    filled = jax.random.randint(key, (ROWS,), CTX // 16, CTX + 1)
    chosen = jax.random.randint(jax.random.fold_in(key, 1), (), 0, ROWS)
    return filled.at[chosen].set(CTX).astype(jnp.int32)


def draw_placement(key, part):
    first = jax.random.permutation(jax.random.fold_in(key, 3), PAIRS)
    second = jax.random.permutation(jax.random.fold_in(key, 4), PAIRS)
    return jnp.stack([first, second]).astype(jnp.int32)


def place_ends(array, key, low, largest):
    spot = [jax.random.randint(jax.random.fold_in(key, axis), (), 0, length) for axis, length in enumerate(array.shape)]
    widest = array.shape.index(max(array.shape))
    beside = spot[:widest] + [(spot[widest] + 1) % array.shape[widest]] + spot[widest + 1:]
    return array.at[tuple(spot)].set(low).at[tuple(beside)].set(largest)


def steps_of(rng, extent, split, least, largest):
    def one(axis_at, blocks):
        heights = jax.random.uniform(jax.random.fold_in(jax.random.fold_in(rng, 6), axis_at), (blocks,), jnp.float32, least / len(split), largest / len(split))
        return jnp.repeat(jnp.exp(heights), extent[axis_at] // blocks).reshape((-1,) + (1,) * (len(extent) - axis_at - 1))

    level = one(*split[0])
    for cut in split[1:]:
        level = level * one(*cut)
    return level


def scatter_about(stream_key, extent, deviation, most, split=(), kind=jnp.bfloat16):
    array = jax.random.normal(stream_key, extent, jnp.float32) * deviation
    if len(split) > 0:
        array = steps_of(stream_key, extent, split, -0.22, 0.18) * array
    return jnp.clip(array, min=-most, max=most).astype(kind)


def setup_inputs(seed: int = 0) -> dict:
    streams_of = jax.random.split(jax.random.key(seed), 15)
    inputs = scatter_about(streams_of[0], (ROWS, D), 1.0, 6.0, ((0, 32),))
    gain_attn = jnp.clip(1.0 + 0.15 * jax.random.normal(streams_of[1], (D,), jnp.float32), 0.25, 1.75)
    w_qkv = scatter_about(streams_of[2], (3, HEADS * HEAD_DIM, D), D ** -0.5, 0.15625, ((1, 8),))
    k_cache = draw_k_cache(jax.random.fold_in(streams_of[14], 71), 0)
    v_cache = scatter_about(streams_of[4], (ROWS, HEADS * HEAD_DIM, CTX), 1.0, 6.0, ((0, 32), (1, 8)))
    lengths = draw_lengths(jax.random.fold_in(streams_of[14], 71), 0)
    pad_mask = place_ends((jax.random.randint(streams_of[6], (ROWS, CTX), 0, 8) < 7).astype(jnp.int32), jax.random.fold_in(streams_of[6], 1), 0, 1)
    w_out = scatter_about(streams_of[7], (HEADS * HEAD_DIM, D), (HEADS * HEAD_DIM) ** -0.5, 0.15625, ((0, 8),))
    gain_mlp = jnp.clip(1.0 + 0.15 * jax.random.normal(streams_of[8], (D,), jnp.float32), 0.25, 1.75)
    w_up = scatter_about(streams_of[9], (FF, D), D ** -0.5, 0.15625, ((0, 8),))
    w_down = scatter_about(streams_of[10], (FF, D), FF ** -0.5, 0.15625, ((0, 8),))
    w_head = scatter_about(streams_of[11], (OUT, D), D ** -0.5, 0.15625, ((0, 8),))
    placement = draw_placement(jax.random.fold_in(streams_of[14], 71), 0)
    guide = jnp.clip(jnp.exp(math.log(6.0) - 1.3862944 * jax.random.uniform(streams_of[13], (PAIRS,), jnp.float32) ** steps_of(streams_of[13], (PAIRS,), ((0, 32),), -0.2, 0.2)), 1.5, 6.0)
    return dict(inputs=inputs, gain_attn=gain_attn, w_qkv=w_qkv, k_cache=k_cache, v_cache=v_cache, lengths=lengths, pad_mask=pad_mask, w_out=w_out, gain_mlp=gain_mlp, w_up=w_up, w_down=w_down, w_head=w_head, placement=placement, guide=guide)


def rms_gain(values, gain):
    return values * lax.rsqrt(lax.optimization_barrier(jnp.mean(values * values, axis=-1, keepdims=True)) + 1e-06) * gain

def project_rows(left, weight):
    return lax.dot_general(left, weight, (((1,), (1,)), ((), ())), preferred_element_type=jnp.float32)

def reference(inputs, gain_attn, w_qkv, k_cache, v_cache, lengths, pad_mask, w_out, gain_mlp, w_up, w_down, w_head, placement, guide):
    width = HEADS * HEAD_DIM
    scale = HEAD_DIM ** (-0.5)
    total_rows = inputs.shape[0]
    xvals = inputs.astype(jnp.float32)
    normed = rms_gain(xvals, gain_attn.astype(jnp.float32)).astype(jnp.bfloat16)
    query = project_rows(normed, w_qkv[0]).astype(jnp.bfloat16)
    key_new = project_rows(normed, w_qkv[1]).astype(jnp.bfloat16)
    value_new = project_rows(normed, w_qkv[2]).astype(jnp.bfloat16)
    query = query.reshape(total_rows, HEADS, HEAD_DIM)
    key_new = key_new.reshape(total_rows, HEADS, HEAD_DIM)
    value_new = value_new.reshape(total_rows, HEADS, HEAD_DIM)

    def attend(items):
        qrow, krow, vrow, kcach, vcach, length, padrow = items
        kc = kcach.reshape(HEADS, HEAD_DIM, CTX).astype(jnp.float32)
        vc = vcach.reshape(HEADS, HEAD_DIM, CTX).astype(jnp.float32)
        qf = qrow.astype(jnp.float32)
        scores = jnp.einsum('hd,hdc->hc', qf, kc) * scale
        valid = (jnp.arange(CTX, dtype=jnp.int32) < length) & (padrow == 1)
        scores = jnp.where(valid[None, :], scores, -1e+30)
        own = lax.optimization_barrier(jnp.sum(qf * krow.astype(jnp.float32), axis=-1)) * scale
        top = jnp.maximum(lax.optimization_barrier(jnp.max(scores, axis=-1)), own)
        expo = jnp.where(valid[None, :], jnp.exp(scores - top[:, None]), 0.0)
        own_exp = jnp.exp(own - top)
        total = lax.optimization_barrier(jnp.sum(expo, axis=-1)) + own_exp
        probs = (expo / total[:, None]).astype(jnp.bfloat16)
        own_prob = (own_exp / total).astype(jnp.bfloat16)
        mixed = jnp.einsum('hc,hdc->hd', probs.astype(jnp.float32), vc)
        mixed = mixed + own_prob.astype(jnp.float32)[:, None] * vrow.astype(jnp.float32)
        return mixed.astype(jnp.bfloat16).reshape(width)
    attn = lax.map(attend, (query, key_new, value_new, k_cache, v_cache, lengths, pad_mask))
    resid = xvals + jnp.dot(attn, w_out, preferred_element_type=jnp.float32)
    normed2 = rms_gain(resid, gain_mlp.astype(jnp.float32)).astype(jnp.bfloat16)
    hidden = jax.nn.gelu(project_rows(normed2, w_up), approximate=True).astype(jnp.bfloat16)
    state = (resid + jnp.dot(hidden, w_down, preferred_element_type=jnp.float32)).astype(jnp.bfloat16)
    head = project_rows(state, w_head)
    cond = head[placement[0]]
    uncond = head[PAIRS + placement[1]]
    return uncond + guide[:, None] * (cond - uncond)
```

```python
import jax
import jax.numpy as jnp
from jax import lax
from jax.sharding import PartitionSpec as P

HEAD_DIM = 80


def rms_gain(values, gain):
    return values * lax.rsqrt(jnp.mean(values * values, axis=-1, keepdims=True) + 1e-06) * gain


def project_rows(left, weight):
    return lax.dot_general(
        left, weight, (((1,), (1,)), ((), ())), preferred_element_type=jnp.float32
    )


def tp_sum(part):
    copies = jnp.broadcast_to(part.astype(jnp.bfloat16)[None], (lax.axis_size("tp"),) + part.shape)
    return jnp.sum(lax.all_to_all(copies, "tp", 0, 0).astype(jnp.float32), axis=0)


def on_device(
    inputs,
    gain_attn,
    w_qkv,
    k_cache,
    v_cache,
    lengths,
    pad_mask,
    w_out,
    gain_mlp,
    w_up,
    w_down,
    w_head,
    placement,
    guide,
):
    rows = inputs.shape[0]
    local_width = w_qkv.shape[1]
    heads_here = local_width // HEAD_DIM
    scale = HEAD_DIM ** (-0.5)
    xvals = inputs.astype(jnp.float32)
    normed = rms_gain(xvals, gain_attn).astype(jnp.bfloat16)
    query = project_rows(normed, w_qkv[0]).astype(jnp.bfloat16).reshape(rows, heads_here, HEAD_DIM)
    key_new = (
        project_rows(normed, w_qkv[1]).astype(jnp.bfloat16).reshape(rows, heads_here, HEAD_DIM)
    )
    value_new = (
        project_rows(normed, w_qkv[2]).astype(jnp.bfloat16).reshape(rows, heads_here, HEAD_DIM)
    )
    own = jnp.sum(query.astype(jnp.float32) * key_new.astype(jnp.float32), axis=-1) * scale
    ctx_slots = k_cache.shape[2]
    block = min(512, ctx_slots)
    offsets = jnp.arange(block, dtype=jnp.int32)
    count = ctx_slots // block

    def score_pass(step, buffer):
        start = step * block
        kblock = lax.dynamic_slice_in_dim(k_cache, start, block, 2).reshape(
            rows, heads_here, HEAD_DIM, block
        )
        scores = (
            jnp.einsum("rhd,rhdb->rhb", query, kblock, preferred_element_type=jnp.float32) * scale
        )
        padrow = lax.dynamic_slice_in_dim(pad_mask, start, block, 1)
        valid = ((start + offsets)[None, :] < lengths[:, None]) & (padrow == 1)
        scores = jnp.where(valid[:, None, :], scores, -1e30)
        return lax.dynamic_update_slice_in_dim(buffer, scores, start, 2)

    empty_scores = jnp.full((rows, heads_here, ctx_slots), -1e30, jnp.float32)
    all_scores = lax.fori_loop(0, count, score_pass, empty_scores)
    top = jnp.maximum(jnp.max(all_scores, axis=-1), own)
    expo = jnp.where(all_scores > -1e29, jnp.exp(all_scores - top[..., None]), 0.0)
    own_exp = jnp.exp(own - top)
    total = jnp.sum(expo, axis=-1) + own_exp
    probs = (expo / total[..., None]).astype(jnp.bfloat16)
    own_prob = (own_exp / total).astype(jnp.bfloat16)

    def value_pass(step, acc):
        start = step * block
        pblock = lax.dynamic_slice_in_dim(probs, start, block, 2)
        vblock = lax.dynamic_slice_in_dim(v_cache, start, block, 2).reshape(
            rows, heads_here, HEAD_DIM, block
        )
        return acc + jnp.einsum("rhb,rhdb->rhd", pblock, vblock, preferred_element_type=jnp.float32)

    start_acc = own_prob.astype(jnp.float32)[..., None] * value_new.astype(jnp.float32)
    attn = (
        lax.fori_loop(0, count, value_pass, start_acc)
        .astype(jnp.bfloat16)
        .reshape(rows, local_width)
    )
    attn_terms = jnp.dot(attn, w_out, preferred_element_type=jnp.float32)
    resid = xvals + tp_sum(attn_terms)
    normed2 = rms_gain(resid, gain_mlp).astype(jnp.bfloat16)
    hidden = jax.nn.gelu(project_rows(normed2, w_up), approximate=True).astype(jnp.bfloat16)
    mlp_terms = jnp.dot(hidden, w_down, preferred_element_type=jnp.float32)
    state = (resid + tp_sum(mlp_terms)).astype(jnp.bfloat16)
    head = project_rows(state, w_head)
    pairs_here = guide.shape[0]
    req_count = lax.axis_size("req")
    half = req_count // 2
    req_index = lax.axis_index("req")
    wanted = jnp.where(req_index < half, placement[0], placement[1])
    mine = (req_index % half) * rows + jnp.arange(rows, dtype=jnp.int32)
    picked = jnp.sum(jnp.where((wanted[:, None] == mine[None, :])[:, :, None], head[None], 0.0), axis=1)
    slots = picked.reshape(req_count, pairs_here, head.shape[1])
    arrived = lax.all_to_all(slots, "req", 0, 0)
    cond = jnp.sum(arrived[:half], axis=0)
    uncond = jnp.sum(arrived[half:], axis=0)
    return uncond + guide[:, None] * (cond - uncond)


def solution(mesh):
    placed = (
        P("req", None),
        P(),
        P(None, "tp", None),
        P("req", "tp", None),
        P("req", "tp", None),
        P("req"),
        P("req", None),
        P("tp", None),
        P(),
        P("tp", None),
        P("tp", None),
        P("tp", None),
        P(),
        P("req"),
    )
    return jax.shard_map(
        on_device, mesh=mesh, in_specs=placed, out_specs=P("req", "tp"), check_vma=False
    )
```

```python
import functools

import jax
import jax.numpy as jnp
from jax import lax
from jax.experimental import pallas as pl
from jax.experimental.pallas import tpu as pltpu
from jax.sharding import PartitionSpec as P

HEAD_DIM = 80
NEG = -1e30
VMEM_BYTES = 40 << 20


def rms_gain(values, gain):
    return values * lax.rsqrt(jnp.mean(values * values, axis=-1, keepdims=True) + 1e-06) * gain


def rows_by_weight(left, weight):
    return lax.dot_general(
        left, weight, (((1,), (1,)), ((), ())), preferred_element_type=jnp.float32
    )


def spread(values, owner, count):
    out = jnp.broadcast_to(values[0:1], owner.shape)
    for r in range(1, count):
        out = jnp.where(owner == r, jnp.broadcast_to(values[r : r + 1], owner.shape), out)
    return out


def attend_kernel(
    x_hbm,
    gain_hbm,
    w_hbm,
    k_hbm,
    v_hbm,
    len_hbm,
    pad_hbm,
    wo_hbm,
    out_ref,
    x_v,
    gain_v,
    w_v,
    k_v,
    v_v,
    len_s,
    pad_v,
    wo_v,
    sems,
):
    rows, width, slots = k_v.shape
    heads = width // HEAD_DIM
    many = rows * heads
    copies = [
        (x_hbm, x_v),
        (gain_hbm, gain_v),
        (w_hbm.at[0], w_v.at[0]),
        (len_hbm, len_s),
        (pad_hbm, pad_v),
    ]
    copies += [(k_hbm.at[r], k_v.at[r]) for r in range(rows)]
    copies += [(w_hbm.at[1], w_v.at[1]), (w_hbm.at[2], w_v.at[2])]
    copies += [(v_hbm.at[r], v_v.at[r]) for r in range(rows)]
    copies += [(wo_hbm, wo_v)]
    flights = [pltpu.make_async_copy(a, b, sems.at[i]) for i, (a, b) in enumerate(copies)]
    for flight in flights:
        flight.start()
    x_in, gain_in, wq_in, len_in, pad_in = flights[:5]
    k_in = flights[5 : 5 + rows]
    wk_in, wv_in = flights[5 + rows : 7 + rows]
    v_in = flights[7 + rows : 7 + 2 * rows]
    wo_in = flights[7 + 2 * rows]
    scale = HEAD_DIM ** (-0.5)

    row_n = lax.broadcasted_iota(jnp.int32, (many, width), 0)
    col_n = lax.broadcasted_iota(jnp.int32, (many, width), 1)
    owner_n = row_n // heads
    own_head = col_n // HEAD_DIM == row_n % heads
    x_in.wait()
    gain_in.wait()
    normed = rms_gain(x_v[...].astype(jnp.float32), gain_v[...]).astype(jnp.bfloat16)

    len_in.wait()
    pad_in.wait()
    row_w = lax.broadcasted_iota(jnp.int32, (many, slots), 0) // heads
    col_w = lax.broadcasted_iota(jnp.int32, (many, slots), 1)
    filled = jnp.full((many, slots), len_s[0], jnp.int32)
    for r in range(1, rows):
        filled = jnp.where(row_w == r, len_s[r], filled)
    valid = (col_w < filled) & (spread(pad_v[...], row_w, rows) == 1)

    def project(which):
        flat = rows_by_weight(normed, w_v[which])
        return spread(flat.astype(jnp.bfloat16).astype(jnp.float32), owner_n, rows)

    wq_in.wait()
    query = jnp.where(own_head, project(0), 0.0)
    scores = None
    for r in range(rows):
        picked = jnp.where(owner_n == r, query, 0.0).astype(jnp.bfloat16)
        k_in[r].wait()
        part = jnp.dot(picked, k_v[r], preferred_element_type=jnp.float32)
        scores = part if scores is None else scores + part
    scores = jnp.where(valid, scores * scale, NEG)
    wk_in.wait()
    own = jnp.sum(query * project(1), axis=1, keepdims=True) * scale
    wv_in.wait()
    value_new = project(2)
    top = jnp.maximum(jnp.max(scores, axis=1, keepdims=True), own)
    expo = jnp.where(valid, jnp.exp(scores - top), 0.0)
    own_exp = jnp.exp(own - top)
    total = jnp.sum(expo, axis=1, keepdims=True) + own_exp
    probs = (expo / total).astype(jnp.bfloat16)
    own_prob = (own_exp / total).astype(jnp.bfloat16).astype(jnp.float32)
    mixed = own_prob * value_new
    for r in range(rows):
        v_in[r].wait()
        mixed = mixed + jnp.where(owner_n == r, rows_by_weight(probs, v_v[r]), 0.0)
    mixed = jnp.where(own_head, mixed, 0.0).astype(jnp.bfloat16).astype(jnp.float32)
    attn = mixed
    for h in range(1, heads):
        attn = attn + pltpu.roll(mixed, many - h, 0)
    wo_in.wait()
    terms = jnp.dot(attn.astype(jnp.bfloat16), wo_v[...], preferred_element_type=jnp.float32)
    terms = jnp.concatenate([terms[r * heads : r * heads + 1] for r in range(rows)], axis=0)
    terms = terms.astype(out_ref.dtype)
    for t in range(out_ref.shape[0]):
        out_ref[t] = terms


def mlp_kernel(parts_ref, x_ref, gain_ref, up_ref, down_ref, out_ref, resid_ref):
    resid = x_ref[...].astype(jnp.float32) + jnp.sum(parts_ref[...].astype(jnp.float32), axis=0)
    resid_ref[...] = resid
    normed = rms_gain(resid, gain_ref[...]).astype(jnp.bfloat16)
    hidden = jax.nn.gelu(rows_by_weight(normed, up_ref[...]), approximate=True)
    terms = jnp.dot(hidden.astype(jnp.bfloat16), down_ref[...], preferred_element_type=jnp.float32)
    terms = terms.astype(out_ref.dtype)
    for t in range(out_ref.shape[0]):
        out_ref[t] = terms


def head_kernel(parts_ref, resid_ref, head_ref, place_ref, out_ref, *, half):
    rows = resid_ref.shape[0]
    pairs = place_ref.shape[1]
    total = jnp.sum(parts_ref[...].astype(jnp.float32), axis=0)
    state = (resid_ref[...] + total).astype(jnp.bfloat16)
    head = rows_by_weight(state, head_ref[...])
    here = lax.axis_index("req")
    place = place_ref[...].astype(jnp.float32)
    wanted = jnp.where(here < half, place[0:1], place[1:2])
    eye = lax.broadcasted_iota(jnp.int32, (pairs, pairs), 0) == lax.broadcasted_iota(
        jnp.int32, (pairs, pairs), 1
    )
    column = jnp.sum(
        jnp.where(eye, jnp.broadcast_to(wanted, (pairs, pairs)), 0.0), axis=1, keepdims=True
    )
    base = ((here % half) * rows).astype(jnp.float32)
    picked = jnp.zeros((pairs, head.shape[1]), jnp.float32)
    for r in range(rows):
        picked = jnp.where(column == base + r, jnp.broadcast_to(head[r : r + 1], picked.shape), picked)
    out_ref[...] = picked.reshape(out_ref.shape)


def whole(count, space):
    return [pl.BlockSpec(memory_space=space)] * count


def tp_exchange(parts):
    return lax.all_to_all(parts, "tp", 0, 0)


def on_device(
    inputs,
    gain_attn,
    w_qkv,
    k_cache,
    v_cache,
    lengths,
    pad_mask,
    w_out,
    gain_mlp,
    w_up,
    w_down,
    w_head,
    placement,
    guide,
):
    rows, model = inputs.shape
    width = w_qkv.shape[1]
    peers = lax.axis_size("tp")
    params = pltpu.CompilerParams(vmem_limit_bytes=VMEM_BYTES)
    parts_shape = jax.ShapeDtypeStruct((peers, rows, model), jnp.bfloat16)
    parts = pl.pallas_call(
        attend_kernel,
        out_shape=parts_shape,
        in_specs=whole(8, pl.ANY),
        out_specs=pl.BlockSpec(memory_space=pltpu.VMEM),
        scratch_shapes=[
            pltpu.VMEM(inputs.shape, inputs.dtype),
            pltpu.VMEM((1, model), jnp.float32),
            pltpu.VMEM(w_qkv.shape, w_qkv.dtype),
            pltpu.VMEM(k_cache.shape, k_cache.dtype),
            pltpu.VMEM(v_cache.shape, v_cache.dtype),
            pltpu.SMEM(lengths.shape, lengths.dtype),
            pltpu.VMEM(pad_mask.shape, pad_mask.dtype),
            pltpu.VMEM(w_out.shape, w_out.dtype),
            pltpu.SemaphoreType.DMA((8 + 2 * rows,)),
        ],
        compiler_params=params,
        name="attend",
    )(inputs, gain_attn[None], w_qkv, k_cache, v_cache, lengths, pad_mask, w_out)
    parts, resid = pl.pallas_call(
        mlp_kernel,
        out_shape=(parts_shape, jax.ShapeDtypeStruct((rows, model), jnp.float32)),
        in_specs=whole(5, pltpu.VMEM),
        out_specs=tuple(whole(2, pltpu.VMEM)),
        compiler_params=params,
        name="mlp",
    )(tp_exchange(parts), inputs, gain_mlp[None], w_up, w_down)
    pairs_here = guide.shape[0]
    devices = lax.axis_size("req")
    slots = pl.pallas_call(
        functools.partial(head_kernel, half=devices // 2),
        out_shape=jax.ShapeDtypeStruct((devices, pairs_here, width), jnp.float32),
        in_specs=whole(4, pltpu.VMEM),
        out_specs=pl.BlockSpec(memory_space=pltpu.VMEM),
        compiler_params=params,
        name="head",
    )(tp_exchange(parts), resid, w_head, placement)
    arrived = lax.all_to_all(slots, "req", 0, 0)
    cond = jnp.sum(arrived[: devices // 2], axis=0)
    uncond = jnp.sum(arrived[devices // 2 :], axis=0)
    return uncond + guide[:, None] * (cond - uncond)


def solution(mesh):
    placed = (
        P("req", None),
        P(),
        P(None, "tp", None),
        P("req", "tp", None),
        P("req", "tp", None),
        P("req"),
        P("req", None),
        P("tp", None),
        P(),
        P("tp", None),
        P("tp", None),
        P("tp", None),
        P(),
        P("req"),
    )
    return jax.shard_map(
        on_device, mesh=mesh, in_specs=placed, out_specs=P("req", "tp"), check_vma=False
    )
```

```python
import functools

import jax
import jax.numpy as jnp
from jax import lax
from jax.experimental import pallas as pl
from jax.experimental.pallas import tpu as pltpu
from jax.sharding import PartitionSpec as P

HEAD_DIM = 80
NEG = -1e30
VMEM_BYTES = 40 << 20


def rms_gain(values, gain):
    return values * lax.rsqrt(jnp.mean(values * values, axis=-1, keepdims=True) + 1e-06) * gain


def rows_by_weight(left, weight):
    return lax.dot_general(
        left, weight, (((1,), (1,)), ((), ())), preferred_element_type=jnp.float32
    )


def spread(values, owner, count):
    out = jnp.broadcast_to(values[0:1], owner.shape)
    for r in range(1, count):
        out = jnp.where(owner == r, jnp.broadcast_to(values[r : r + 1], owner.shape), out)
    return out


def attend_kernel(
    x_hbm,
    gain_hbm,
    w_hbm,
    k_hbm,
    v_hbm,
    len_hbm,
    pad_hbm,
    wo_hbm,
    out_ref,
    x_v,
    gain_v,
    w_v,
    k_v,
    v_v,
    len_s,
    pad_v,
    wo_v,
    sems,
):
    rows, width, slots = k_v.shape
    heads = width // HEAD_DIM
    many = rows * heads
    copies = [
        (x_hbm, x_v),
        (gain_hbm, gain_v),
        (w_hbm.at[0], w_v.at[0]),
        (len_hbm, len_s),
        (pad_hbm, pad_v),
    ]
    copies += [(k_hbm.at[r], k_v.at[r]) for r in range(rows)]
    copies += [(w_hbm.at[1], w_v.at[1]), (w_hbm.at[2], w_v.at[2])]
    copies += [(v_hbm.at[r], v_v.at[r]) for r in range(rows)]
    copies += [(wo_hbm, wo_v)]
    flights = [pltpu.make_async_copy(a, b, sems.at[i]) for i, (a, b) in enumerate(copies)]
    for flight in flights:
        flight.start()
    x_in, gain_in, wq_in, len_in, pad_in = flights[:5]
    k_in = flights[5 : 5 + rows]
    wk_in, wv_in = flights[5 + rows : 7 + rows]
    v_in = flights[7 + rows : 7 + 2 * rows]
    wo_in = flights[7 + 2 * rows]
    scale = HEAD_DIM ** (-0.5)

    row_n = lax.broadcasted_iota(jnp.int32, (many, width), 0)
    col_n = lax.broadcasted_iota(jnp.int32, (many, width), 1)
    owner_n = row_n // heads
    own_head = col_n // HEAD_DIM == row_n % heads
    x_in.wait()
    gain_in.wait()
    normed = rms_gain(x_v[...].astype(jnp.float32), gain_v[...][None]).astype(jnp.bfloat16)

    len_in.wait()
    pad_in.wait()
    row_w = lax.broadcasted_iota(jnp.int32, (many, slots), 0) // heads
    col_w = lax.broadcasted_iota(jnp.int32, (many, slots), 1)
    filled = jnp.full((many, slots), len_s[0], jnp.int32)
    for r in range(1, rows):
        filled = jnp.where(row_w == r, len_s[r], filled)
    valid = (col_w < filled) & (spread(pad_v[...], row_w, rows) == 1)

    def project(which):
        flat = rows_by_weight(normed, w_v[which])
        return spread(flat.astype(jnp.bfloat16).astype(jnp.float32), owner_n, rows)

    wq_in.wait()
    query = jnp.where(own_head, project(0), 0.0)
    scores = None
    for r in range(rows):
        picked = jnp.where(owner_n == r, query, 0.0).astype(jnp.bfloat16)
        k_in[r].wait()
        part = jnp.dot(picked, k_v[r], preferred_element_type=jnp.float32)
        scores = part if scores is None else scores + part
    scores = jnp.where(valid, scores * scale, NEG)
    wk_in.wait()
    own = jnp.sum(query * project(1), axis=1, keepdims=True) * scale
    wv_in.wait()
    value_new = project(2)
    top = jnp.maximum(jnp.max(scores, axis=1, keepdims=True), own)
    expo = jnp.where(valid, jnp.exp(scores - top), 0.0)
    own_exp = jnp.exp(own - top)
    total = jnp.sum(expo, axis=1, keepdims=True) + own_exp
    probs = (expo / total).astype(jnp.bfloat16)
    own_prob = (own_exp / total).astype(jnp.bfloat16).astype(jnp.float32)
    mixed = own_prob * value_new
    for r in range(rows):
        v_in[r].wait()
        mixed = mixed + jnp.where(owner_n == r, rows_by_weight(probs, v_v[r]), 0.0)
    mixed = jnp.where(own_head, mixed, 0.0).astype(jnp.bfloat16).astype(jnp.float32)
    attn = mixed
    for h in range(1, heads):
        attn = attn + pltpu.roll(mixed, many - h, 0)
    wo_in.wait()
    terms = jnp.dot(attn.astype(jnp.bfloat16), wo_v[...], preferred_element_type=jnp.float32)
    terms = jnp.concatenate([terms[r * heads : r * heads + 1] for r in range(rows)], axis=0)
    terms = terms.astype(out_ref.dtype)
    for t in range(out_ref.shape[0]):
        out_ref[t] = terms


def mlp_kernel(parts_ref, x_ref, gain_ref, up_ref, down_ref, out_ref, resid_ref):
    resid = x_ref[...].astype(jnp.float32) + jnp.sum(parts_ref[...].astype(jnp.float32), axis=0)
    resid_ref[...] = resid
    normed = rms_gain(resid, gain_ref[...][None]).astype(jnp.bfloat16)
    hidden = jax.nn.gelu(rows_by_weight(normed, up_ref[...]), approximate=True)
    terms = jnp.dot(hidden.astype(jnp.bfloat16), down_ref[...], preferred_element_type=jnp.float32)
    terms = terms.astype(out_ref.dtype)
    for t in range(out_ref.shape[0]):
        out_ref[t] = terms


def head_kernel(parts_ref, resid_ref, head_ref, place_ref, out_ref, *, half):
    rows = resid_ref.shape[0]
    pairs = place_ref.shape[1]
    total = jnp.sum(parts_ref[...].astype(jnp.float32), axis=0)
    state = (resid_ref[...] + total).astype(jnp.bfloat16)
    head = rows_by_weight(state, head_ref[...])
    here = lax.axis_index("req")
    place = place_ref[...].astype(jnp.float32)
    wanted = jnp.where(here < half, place[0:1], place[1:2])
    eye = lax.broadcasted_iota(jnp.int32, (pairs, pairs), 0) == lax.broadcasted_iota(
        jnp.int32, (pairs, pairs), 1
    )
    column = jnp.sum(
        jnp.where(eye, jnp.broadcast_to(wanted, (pairs, pairs)), 0.0), axis=1, keepdims=True
    )
    base = ((here % half) * rows).astype(jnp.float32)
    picked = jnp.zeros((pairs, head.shape[1]), jnp.float32)
    for r in range(rows):
        picked = jnp.where(column == base + r, jnp.broadcast_to(head[r : r + 1], picked.shape), picked)
    out_ref[...] = picked.reshape(out_ref.shape)


def whole(count, space):
    return [pl.BlockSpec(memory_space=space)] * count


def tp_exchange(parts):
    return lax.all_to_all(parts, "tp", 0, 0)


def on_device(
    inputs,
    gain_attn,
    w_qkv,
    k_cache,
    v_cache,
    lengths,
    pad_mask,
    w_out,
    gain_mlp,
    w_up,
    w_down,
    w_head,
    placement,
    guide,
):
    rows, model = inputs.shape
    width = w_qkv.shape[1]
    peers = lax.axis_size("tp")
    params = pltpu.CompilerParams(vmem_limit_bytes=VMEM_BYTES)
    parts_shape = jax.ShapeDtypeStruct((peers, rows, model), jnp.bfloat16)
    parts = pl.pallas_call(
        attend_kernel,
        out_shape=parts_shape,
        in_specs=whole(8, pltpu.HBM),
        out_specs=pl.BlockSpec(memory_space=pltpu.VMEM),
        scratch_shapes=[
            pltpu.VMEM(inputs.shape, inputs.dtype),
            pltpu.VMEM((model,), jnp.float32),
            pltpu.VMEM(w_qkv.shape, w_qkv.dtype),
            pltpu.VMEM(k_cache.shape, k_cache.dtype),
            pltpu.VMEM(v_cache.shape, v_cache.dtype),
            pltpu.SMEM(lengths.shape, lengths.dtype),
            pltpu.VMEM(pad_mask.shape, pad_mask.dtype),
            pltpu.VMEM(w_out.shape, w_out.dtype),
            pltpu.SemaphoreType.DMA((8 + 2 * rows,)),
        ],
        compiler_params=params,
        name="attend",
    )(*[pltpu.with_memory_space_constraint(a, pltpu.HBM) for a in (inputs, gain_attn, w_qkv, k_cache, v_cache, lengths, pad_mask, w_out)])
    parts, resid = pl.pallas_call(
        mlp_kernel,
        out_shape=(parts_shape, jax.ShapeDtypeStruct((rows, model), jnp.float32)),
        in_specs=whole(5, pltpu.VMEM),
        out_specs=tuple(whole(2, pltpu.VMEM)),
        compiler_params=params,
        name="mlp",
    )(tp_exchange(parts), inputs, gain_mlp, w_up, w_down)
    pairs_here = guide.shape[0]
    devices = lax.axis_size("req")
    slots = pl.pallas_call(
        functools.partial(head_kernel, half=devices // 2),
        out_shape=jax.ShapeDtypeStruct((devices, pairs_here, width), jnp.float32),
        in_specs=whole(4, pltpu.VMEM),
        out_specs=pl.BlockSpec(memory_space=pltpu.VMEM),
        compiler_params=params,
        name="head",
    )(tp_exchange(parts), resid, w_head, placement)
    arrived = lax.all_to_all(slots, "req", 0, 0)
    cond = jnp.sum(arrived[: devices // 2], axis=0)
    uncond = jnp.sum(arrived[devices // 2 :], axis=0)
    return uncond + guide[:, None] * (cond - uncond)


def solution(mesh):
    placed = (
        P("req", None),
        P(),
        P(None, "tp", None),
        P("req", "tp", None),
        P("req", "tp", None),
        P("req"),
        P("req", None),
        P("tp", None),
        P(),
        P("tp", None),
        P("tp", None),
        P("tp", None),
        P(),
        P("req"),
    )
    return jax.shard_map(
        on_device, mesh=mesh, in_specs=placed, out_specs=P("req", "tp"), check_vma=False
    )
```

```python
import functools

import jax
import jax.numpy as jnp
from jax import lax
from jax.experimental import pallas as pl
from jax.experimental.pallas import tpu as pltpu
from jax.sharding import PartitionSpec as P

HEAD_DIM = 80
NEG = -1e30
LANES = 128
BATCHES = 2
VMEM_BYTES = 40 << 20


def rms_gain(values, gain):
    return values * lax.rsqrt(jnp.mean(values * values, axis=-1, keepdims=True) + 1e-06) * gain


def rows_by_weight(left, weight):
    return lax.dot_general(
        left, weight, (((1,), (1,)), ((), ())), preferred_element_type=jnp.float32
    )


def spread(values, owner, count):
    out = jnp.broadcast_to(values[0:1], owner.shape)
    for r in range(1, count):
        out = jnp.where(owner == r, jnp.broadcast_to(values[r : r + 1], owner.shape), out)
    return out


def attend_kernel(
    x_hbm,
    gain_hbm,
    w_hbm,
    k_hbm,
    v_hbm,
    len_hbm,
    pad_hbm,
    wo_hbm,
    out_ref,
    x_v,
    gain_v,
    w_v,
    k_v,
    v_v,
    len_s,
    pad_v,
    wo_v,
    sems,
):
    rows, width, slots = k_v.shape
    heads = width // HEAD_DIM
    many = rows * heads
    group = rows // BATCHES
    copies = [
        (x_hbm, x_v),
        (gain_hbm, gain_v),
        (len_hbm, len_s),
        (pad_hbm, pad_v),
        (w_hbm, w_v),
    ]
    for a, b in ((k_hbm, k_v), (v_hbm, v_v)):
        for i in range(BATCHES):
            part = pl.ds(i * group, group)
            copies.append((a.at[part], b.at[part]))
    copies.append((wo_hbm, wo_v))
    flights = [pltpu.make_async_copy(a, b, sems.at[i]) for i, (a, b) in enumerate(copies)]
    for flight in flights:
        flight.start()
    w_in = flights[4]
    k_in = flights[5 : 5 + BATCHES]
    v_in = flights[5 + BATCHES : 5 + 2 * BATCHES]
    wo_in = flights[5 + 2 * BATCHES]
    scale = HEAD_DIM ** (-0.5)

    owner = lax.broadcasted_iota(jnp.int32, (many, width), 0) // heads
    which = lax.broadcasted_iota(jnp.int32, (many, width), 0) % heads
    own_head = lax.broadcasted_iota(jnp.int32, (many, width), 1) // HEAD_DIM == which
    for flight in flights[:4]:
        flight.wait()
    normed = rms_gain(x_v[...].astype(jnp.float32), gain_v[...][None]).astype(jnp.bfloat16)
    owner_slot = lax.broadcasted_iota(jnp.int32, (many, slots), 0) // heads
    filled = jnp.full((many, slots), len_s[0], jnp.int32)
    for r in range(1, rows):
        filled = jnp.where(owner_slot == r, len_s[r], filled)
    valid = lax.broadcasted_iota(jnp.int32, (many, slots), 1) < filled
    valid = valid & (spread(pad_v[...], owner_slot, rows) == 1)

    w_in.wait()
    fused = rows_by_weight(normed, w_v[...]).astype(jnp.bfloat16).astype(jnp.float32)
    fused = spread(fused, lax.broadcasted_iota(jnp.int32, (many, 3 * width), 0) // heads, rows)
    query = jnp.where(own_head, fused[:, :width], 0.0)
    key_new = fused[:, width : 2 * width]
    value_new = fused[:, 2 * width :]
    own = jnp.sum(query * key_new, axis=1, keepdims=True) * scale
    scores = None
    for r in range(rows):
        if r % group == 0:
            k_in[r // group].wait()
        picked = jnp.where(owner == r, query, 0.0).astype(jnp.bfloat16)
        part = jnp.dot(picked, k_v[r], preferred_element_type=jnp.float32)
        scores = part if scores is None else scores + part
    scores = jnp.where(valid, scores * scale, NEG)
    top = jnp.maximum(jnp.max(scores, axis=1, keepdims=True), own)
    expo = jnp.where(valid, jnp.exp(scores - top), 0.0)
    own_exp = jnp.exp(own - top)
    inverse = 1.0 / (jnp.sum(expo, axis=1, keepdims=True) + own_exp)
    probs = (expo * inverse).astype(jnp.bfloat16).astype(jnp.float32)
    own_prob = (own_exp * inverse).astype(jnp.bfloat16).astype(jnp.float32)
    fresh = jnp.where(own_head, own_prob * value_new, 0.0)
    mixed = fresh
    for h in range(1, heads):
        mixed = mixed + pltpu.roll(fresh, many - h, 0)
    mixed = jnp.concatenate([mixed[r * heads : r * heads + 1] for r in range(rows)], axis=0)

    lane = lax.broadcasted_iota(jnp.int32, (width, LANES), 1)
    columns = jnp.zeros((width, LANES), jnp.float32)
    for r in range(rows):
        if r % group == 0:
            v_in[r // group].wait()
        sums = []
        for h in range(heads):
            weights = probs[r * heads + h : r * heads + h + 1]
            acc = None
            for c in range(0, slots, LANES):
                block = v_v[r, pl.ds(h * HEAD_DIM, HEAD_DIM), pl.ds(c, LANES)].astype(jnp.float32)
                block = block * weights[:, c : c + LANES]
                acc = block if acc is None else acc + block
            sums.append(acc)
        column = jnp.sum(jnp.concatenate(sums, axis=0), axis=1, keepdims=True)
        columns = jnp.where(lane == r, column, columns)
    attn = (mixed + columns.T[:rows]).astype(jnp.bfloat16)
    wo_in.wait()
    terms = jnp.dot(attn, wo_v[...], preferred_element_type=jnp.float32).astype(out_ref.dtype)
    for t in range(out_ref.shape[0]):
        out_ref[t] = terms


def mlp_kernel(parts_ref, x_ref, gain_ref, up_ref, down_ref, out_ref, resid_ref):
    resid = x_ref[...].astype(jnp.float32) + jnp.sum(parts_ref[...].astype(jnp.float32), axis=0)
    resid_ref[...] = resid
    inverse = lax.rsqrt(jnp.mean(resid * resid, axis=-1, keepdims=True) + 1e-06)
    scaled = (resid * gain_ref[...][None]).astype(jnp.bfloat16)
    hidden = jax.nn.gelu(rows_by_weight(scaled, up_ref[...]) * inverse, approximate=True)
    terms = jnp.dot(hidden.astype(jnp.bfloat16), down_ref[...], preferred_element_type=jnp.float32)
    terms = terms.astype(out_ref.dtype)
    for t in range(out_ref.shape[0]):
        out_ref[t] = terms


def head_kernel(parts_ref, resid_ref, head_ref, place_ref, out_ref, *, half):
    rows = resid_ref.shape[0]
    pairs = place_ref.shape[1]
    total = jnp.sum(parts_ref[...].astype(jnp.float32), axis=0)
    state = (resid_ref[...] + total).astype(jnp.bfloat16)
    head = rows_by_weight(state, head_ref[...])
    here = lax.axis_index("req")
    place = place_ref[...].astype(jnp.float32)
    wanted = jnp.where(here < half, place[0:1], place[1:2])
    eye = lax.broadcasted_iota(jnp.int32, (pairs, pairs), 0) == lax.broadcasted_iota(
        jnp.int32, (pairs, pairs), 1
    )
    column = jnp.sum(
        jnp.where(eye, jnp.broadcast_to(wanted, (pairs, pairs)), 0.0), axis=1, keepdims=True
    )
    base = ((here % half) * rows).astype(jnp.float32)
    picked = jnp.zeros((pairs, head.shape[1]), jnp.float32)
    for r in range(rows):
        picked = jnp.where(column == base + r, jnp.broadcast_to(head[r : r + 1], picked.shape), picked)
    out_ref[...] = picked.reshape(out_ref.shape)


def whole(count, space):
    return [pl.BlockSpec(memory_space=space)] * count


def tp_exchange(parts):
    return lax.all_to_all(parts, "tp", 0, 0)


def on_device(
    inputs,
    gain_attn,
    w_qkv,
    k_cache,
    v_cache,
    lengths,
    pad_mask,
    w_out,
    gain_mlp,
    w_up,
    w_down,
    w_head,
    placement,
    guide,
):
    rows, model = inputs.shape
    width = w_qkv.shape[1]
    peers = lax.axis_size("tp")
    params = pltpu.CompilerParams(vmem_limit_bytes=VMEM_BYTES)
    parts_shape = jax.ShapeDtypeStruct((peers, rows, model), jnp.bfloat16)
    fused = w_qkv.reshape(-1, model)
    operands = (inputs, gain_attn, fused, k_cache, v_cache, lengths, pad_mask, w_out)
    parts = pl.pallas_call(
        attend_kernel,
        out_shape=parts_shape,
        in_specs=whole(8, pltpu.HBM),
        out_specs=pl.BlockSpec(memory_space=pltpu.VMEM),
        scratch_shapes=[
            pltpu.VMEM(inputs.shape, inputs.dtype),
            pltpu.VMEM((model,), jnp.float32),
            pltpu.VMEM(fused.shape, fused.dtype),
            pltpu.VMEM(k_cache.shape, k_cache.dtype),
            pltpu.VMEM(v_cache.shape, v_cache.dtype),
            pltpu.SMEM(lengths.shape, lengths.dtype),
            pltpu.VMEM(pad_mask.shape, pad_mask.dtype),
            pltpu.VMEM(w_out.shape, w_out.dtype),
            pltpu.SemaphoreType.DMA((6 + 2 * BATCHES,)),
        ],
        compiler_params=params,
        name="attend",
    )(*(pltpu.with_memory_space_constraint(a, pltpu.HBM) for a in operands))
    parts, resid = pl.pallas_call(
        mlp_kernel,
        out_shape=(parts_shape, jax.ShapeDtypeStruct((rows, model), jnp.float32)),
        in_specs=whole(5, pltpu.VMEM),
        out_specs=tuple(whole(2, pltpu.VMEM)),
        compiler_params=params,
        name="mlp",
    )(tp_exchange(parts), inputs, gain_mlp, w_up, w_down)
    pairs_here = guide.shape[0]
    devices = lax.axis_size("req")
    slots = pl.pallas_call(
        functools.partial(head_kernel, half=devices // 2),
        out_shape=jax.ShapeDtypeStruct((devices, pairs_here, width), jnp.float32),
        in_specs=whole(4, pltpu.VMEM),
        out_specs=pl.BlockSpec(memory_space=pltpu.VMEM),
        compiler_params=params,
        name="head",
    )(tp_exchange(parts), resid, w_head, placement)
    arrived = lax.all_to_all(slots, "req", 0, 0)
    cond = jnp.sum(arrived[: devices // 2], axis=0)
    uncond = jnp.sum(arrived[devices // 2 :], axis=0)
    return uncond + guide[:, None] * (cond - uncond)


def solution(mesh):
    placed = (
        P("req", None),
        P(),
        P(None, "tp", None),
        P("req", "tp", None),
        P("req", "tp", None),
        P("req"),
        P("req", None),
        P("tp", None),
        P(),
        P("tp", None),
        P("tp", None),
        P("tp", None),
        P(),
        P("req"),
    )
    return jax.shard_map(
        on_device, mesh=mesh, in_specs=placed, out_specs=P("req", "tp"), check_vma=False
    )
```

```python
import functools

import jax
import jax.numpy as jnp
from jax import lax
from jax.experimental import pallas as pl
from jax.experimental.pallas import tpu as pltpu
from jax.sharding import PartitionSpec as P

HEAD_DIM = 80
NEG = -1e30
LANES = 128
BATCHES = 2
VMEM_BYTES = 40 << 20


def rms_gain(values, gain):
    return values * lax.rsqrt(jnp.mean(values * values, axis=-1, keepdims=True) + 1e-06) * gain


def rows_by_weight(left, weight):
    return lax.dot_general(
        left, weight, (((1,), (1,)), ((), ())), preferred_element_type=jnp.float32
    )


def spread(values, owner, count):
    out = jnp.broadcast_to(values[0:1], owner.shape)
    for r in range(1, count):
        out = jnp.where(owner == r, jnp.broadcast_to(values[r : r + 1], owner.shape), out)
    return out


def attend_kernel(
    x_hbm,
    gain_hbm,
    w_hbm,
    k_hbm,
    v_hbm,
    len_hbm,
    pad_hbm,
    wo_hbm,
    out_ref,
    x_v,
    gain_v,
    w_v,
    k_v,
    v_v,
    len_s,
    pad_v,
    wo_v,
    sems,
):
    rows, width, slots = k_v.shape
    heads = width // HEAD_DIM
    many = rows * heads
    group = rows // BATCHES
    copies = [
        (x_hbm, x_v),
        (gain_hbm, gain_v),
        (len_hbm, len_s),
        (pad_hbm, pad_v),
        (w_hbm, w_v),
    ]
    for a, b in ((k_hbm, k_v), (v_hbm, v_v)):
        for i in range(BATCHES):
            part = pl.ds(i * group, group)
            copies.append((a.at[part], b.at[part]))
    copies.append((wo_hbm, wo_v))
    flights = [pltpu.make_async_copy(a, b, sems.at[i]) for i, (a, b) in enumerate(copies)]
    for flight in flights:
        flight.start()
    w_in = flights[4]
    k_in = flights[5 : 5 + BATCHES]
    v_in = flights[5 + BATCHES : 5 + 2 * BATCHES]
    wo_in = flights[5 + 2 * BATCHES]
    scale = HEAD_DIM ** (-0.5)

    owner = lax.broadcasted_iota(jnp.int32, (many, width), 0) // heads
    which = lax.broadcasted_iota(jnp.int32, (many, width), 0) % heads
    own_head = lax.broadcasted_iota(jnp.int32, (many, width), 1) // HEAD_DIM == which
    for flight in flights[:4]:
        flight.wait()
    normed = rms_gain(x_v[...].astype(jnp.float32), gain_v[...][None]).astype(jnp.bfloat16)
    owner_slot = lax.broadcasted_iota(jnp.int32, (many, slots), 0) // heads
    filled = jnp.full((many, slots), len_s[0], jnp.int32)
    for r in range(1, rows):
        filled = jnp.where(owner_slot == r, len_s[r], filled)
    valid = lax.broadcasted_iota(jnp.int32, (many, slots), 1) < filled
    valid = valid & (spread(pad_v[...], owner_slot, rows) == 1)

    w_in.wait()
    fused = rows_by_weight(normed, w_v[...]).astype(jnp.bfloat16).astype(jnp.float32)
    fused = spread(fused, lax.broadcasted_iota(jnp.int32, (many, 3 * width), 0) // heads, rows)
    query = jnp.where(own_head, fused[:, :width], 0.0)
    key_new = fused[:, width : 2 * width]
    value_new = fused[:, 2 * width :]
    own = jnp.sum(query * key_new, axis=1, keepdims=True) * scale
    scores = None
    for r in range(rows):
        if r % group == 0:
            k_in[r // group].wait()
        picked = jnp.where(owner == r, query, 0.0).astype(jnp.bfloat16)
        part = jnp.dot(picked, k_v[r], preferred_element_type=jnp.float32)
        scores = part if scores is None else scores + part
    scores = jnp.where(valid, scores * scale, NEG)
    top = jnp.maximum(jnp.max(scores, axis=1, keepdims=True), own)
    expo = jnp.where(valid, jnp.exp(scores - top), 0.0)
    own_exp = jnp.exp(own - top)
    inverse = 1.0 / (jnp.sum(expo, axis=1, keepdims=True) + own_exp)
    probs = (expo * inverse).astype(jnp.bfloat16).astype(jnp.float32)
    own_prob = (own_exp * inverse).astype(jnp.bfloat16).astype(jnp.float32)
    fresh = jnp.where(own_head, own_prob * value_new, 0.0)
    mixed = fresh
    for h in range(1, heads):
        mixed = mixed + pltpu.roll(fresh, many - h, 0)
    mixed = jnp.concatenate([mixed[r * heads : r * heads + 1] for r in range(rows)], axis=0)

    lane = lax.broadcasted_iota(jnp.int32, (width, LANES), 1)
    columns = jnp.zeros((width, LANES), jnp.float32)
    for r in range(rows):
        if r % group == 0:
            v_in[r // group].wait()
        sums = []
        for h in range(heads):
            weights = probs[r * heads + h : r * heads + h + 1]
            acc = None
            for c in range(0, slots, LANES):
                block = v_v[r, pl.ds(h * HEAD_DIM, HEAD_DIM), pl.ds(c, LANES)].astype(jnp.float32)
                block = block * weights[:, c : c + LANES]
                acc = block if acc is None else acc + block
            sums.append(acc)
        column = jnp.sum(jnp.concatenate(sums, axis=0), axis=1, keepdims=True)
        columns = jnp.where(lane == r, column, columns)
    attn = (mixed + columns.T[:rows]).astype(jnp.bfloat16)
    wo_in.wait()
    terms = jnp.dot(attn, wo_v[...], preferred_element_type=jnp.float32).astype(out_ref.dtype)
    for t in range(out_ref.shape[0]):
        out_ref[t] = terms


def mlp_kernel(parts_ref, x_ref, gain_ref, up_ref, down_ref, out_ref, resid_ref):
    resid = x_ref[...].astype(jnp.float32) + jnp.sum(parts_ref[...].astype(jnp.float32), axis=0)
    resid_ref[...] = resid
    inverse = lax.rsqrt(jnp.mean(resid * resid, axis=-1, keepdims=True) + 1e-06)
    scaled = (resid * gain_ref[...][None]).astype(jnp.bfloat16)
    hidden = jax.nn.gelu(rows_by_weight(scaled, up_ref[...]) * inverse, approximate=True)
    terms = jnp.dot(hidden.astype(jnp.bfloat16), down_ref[...], preferred_element_type=jnp.float32)
    terms = terms.astype(out_ref.dtype)
    for t in range(out_ref.shape[0]):
        out_ref[t] = terms


def head_kernel(parts_ref, resid_ref, head_ref, place_ref, out_ref, *, half):
    rows = resid_ref.shape[0]
    pairs = place_ref.shape[1]
    total = jnp.sum(parts_ref[...].astype(jnp.float32), axis=0)
    state = (resid_ref[...] + total).astype(jnp.bfloat16)
    head = rows_by_weight(state, head_ref[...])
    here = lax.axis_index("req")
    place = place_ref[...].astype(jnp.float32)
    wanted = jnp.where(here < half, place[0:1], place[1:2])
    eye = lax.broadcasted_iota(jnp.int32, (pairs, pairs), 0) == lax.broadcasted_iota(
        jnp.int32, (pairs, pairs), 1
    )
    column = jnp.sum(
        jnp.where(eye, jnp.broadcast_to(wanted, (pairs, pairs)), 0.0), axis=1, keepdims=True
    )
    base = ((here % half) * rows).astype(jnp.float32)
    picked = jnp.zeros((pairs, head.shape[1]), jnp.float32)
    for r in range(rows):
        picked = jnp.where(column == base + r, jnp.broadcast_to(head[r : r + 1], picked.shape), picked)
    out_ref[...] = picked.reshape(out_ref.shape)


def guide_kernel(arrived_ref, guide_ref, out_ref, value_v, sem, *, half):
    cond = jnp.sum(arrived_ref[:half], axis=0)
    uncond = jnp.sum(arrived_ref[half:], axis=0)
    weights = guide_ref[...][None]
    row = lax.broadcasted_iota(jnp.int32, cond.shape, 0)
    weight = jnp.broadcast_to(weights[:, 0:1], cond.shape)
    for j in range(1, cond.shape[0]):
        weight = jnp.where(row == j, jnp.broadcast_to(weights[:, j : j + 1], cond.shape), weight)
    value_v[...] = uncond + weight * (cond - uncond)
    copy = pltpu.make_async_copy(value_v, out_ref, sem)
    copy.start()
    copy.wait()


def whole(count, space):
    return [pl.BlockSpec(memory_space=space)] * count


def tp_exchange(parts):
    return lax.all_to_all(parts, "tp", 0, 0)


def on_device(
    inputs,
    gain_attn,
    w_qkv,
    k_cache,
    v_cache,
    lengths,
    pad_mask,
    w_out,
    gain_mlp,
    w_up,
    w_down,
    w_head,
    placement,
    guide,
):
    rows, model = inputs.shape
    width = w_qkv.shape[1]
    peers = lax.axis_size("tp")
    params = pltpu.CompilerParams(vmem_limit_bytes=VMEM_BYTES)
    parts_shape = jax.ShapeDtypeStruct((peers, rows, model), jnp.bfloat16)
    fused = w_qkv.reshape(-1, model)
    operands = (inputs, gain_attn, fused, k_cache, v_cache, lengths, pad_mask, w_out)
    parts = pl.pallas_call(
        attend_kernel,
        out_shape=parts_shape,
        in_specs=whole(8, pltpu.HBM),
        out_specs=pl.BlockSpec(memory_space=pltpu.VMEM),
        scratch_shapes=[
            pltpu.VMEM(inputs.shape, inputs.dtype),
            pltpu.VMEM((model,), jnp.float32),
            pltpu.VMEM(fused.shape, fused.dtype),
            pltpu.VMEM(k_cache.shape, k_cache.dtype),
            pltpu.VMEM(v_cache.shape, v_cache.dtype),
            pltpu.SMEM(lengths.shape, lengths.dtype),
            pltpu.VMEM(pad_mask.shape, pad_mask.dtype),
            pltpu.VMEM(w_out.shape, w_out.dtype),
            pltpu.SemaphoreType.DMA((6 + 2 * BATCHES,)),
        ],
        compiler_params=params,
        name="attend",
    )(*(pltpu.with_memory_space_constraint(a, pltpu.HBM) for a in operands))
    parts, resid = pl.pallas_call(
        mlp_kernel,
        out_shape=(parts_shape, jax.ShapeDtypeStruct((rows, model), jnp.float32)),
        in_specs=whole(5, pltpu.VMEM),
        out_specs=tuple(whole(2, pltpu.VMEM)),
        compiler_params=params,
        name="mlp",
    )(tp_exchange(parts), inputs, gain_mlp, w_up, w_down)
    pairs_here = guide.shape[0]
    devices = lax.axis_size("req")
    slots = pl.pallas_call(
        functools.partial(head_kernel, half=devices // 2),
        out_shape=jax.ShapeDtypeStruct((devices, pairs_here, width), jnp.float32),
        in_specs=whole(4, pltpu.VMEM),
        out_specs=pl.BlockSpec(memory_space=pltpu.VMEM),
        compiler_params=params,
        name="head",
    )(tp_exchange(parts), resid, w_head, placement)
    arrived = lax.all_to_all(slots, "req", 0, 0)
    return pl.pallas_call(
        functools.partial(guide_kernel, half=devices // 2),
        out_shape=jax.ShapeDtypeStruct((pairs_here, width), jnp.float32),
        in_specs=whole(2, pltpu.VMEM),
        out_specs=pl.BlockSpec(memory_space=pltpu.HBM),
        scratch_shapes=[
            pltpu.VMEM((pairs_here, width), jnp.float32),
            pltpu.SemaphoreType.DMA(()),
        ],
        compiler_params=params,
        name="guide",
    )(arrived, guide)


def solution(mesh):
    placed = (
        P("req", None),
        P(),
        P(None, "tp", None),
        P("req", "tp", None),
        P("req", "tp", None),
        P("req"),
        P("req", None),
        P("tp", None),
        P(),
        P("tp", None),
        P("tp", None),
        P("tp", None),
        P(),
        P("req"),
    )
    return jax.shard_map(
        on_device, mesh=mesh, in_specs=placed, out_specs=P("req", "tp"), check_vma=False
    )
```

```python
import functools

import jax
import jax.numpy as jnp
from jax import lax
from jax.experimental import pallas as pl
from jax.experimental.pallas import tpu as pltpu
from jax.sharding import PartitionSpec as P

HEAD_DIM = 80
NEG = -1e30
LANES = 128
BATCHES = 2
VMEM_BYTES = 40 << 20


def rms_gain(values, gain):
    return values * lax.rsqrt(jnp.mean(values * values, axis=-1, keepdims=True) + 1e-06) * gain


def rows_by_weight(left, weight):
    return lax.dot_general(
        left, weight, (((1,), (1,)), ((), ())), preferred_element_type=jnp.float32
    )


def spread(values, owner, count):
    out = jnp.broadcast_to(values[0:1], owner.shape)
    for r in range(1, count):
        out = jnp.where(owner == r, jnp.broadcast_to(values[r : r + 1], owner.shape), out)
    return out


def attend_kernel(
    x_hbm,
    gain_hbm,
    w_hbm,
    k_hbm,
    v_hbm,
    len_hbm,
    pad_hbm,
    wo_hbm,
    up_hbm,
    down_hbm,
    head_hbm,
    out_ref,
    up_ref,
    down_ref,
    head_ref,
    x_v,
    gain_v,
    w_v,
    k_v,
    v_v,
    len_s,
    pad_v,
    wo_v,
    sems,
):
    rows, width, slots = k_v.shape
    heads = width // HEAD_DIM
    many = rows * heads
    group = rows // BATCHES
    copies = [
        (x_hbm, x_v),
        (gain_hbm, gain_v),
        (len_hbm, len_s),
        (pad_hbm, pad_v),
        (w_hbm, w_v),
    ]
    for a, b in ((k_hbm, k_v), (v_hbm, v_v)):
        for i in range(BATCHES):
            part = pl.ds(i * group, group)
            copies.append((a.at[part], b.at[part]))
    copies.append((wo_hbm, wo_v))
    copies += [(up_hbm, up_ref), (down_hbm, down_ref), (head_hbm, head_ref)]
    flights = [pltpu.make_async_copy(a, b, sems.at[i]) for i, (a, b) in enumerate(copies)]
    for flight in flights:
        flight.start()
    w_in = flights[4]
    k_in = flights[5 : 5 + BATCHES]
    v_in = flights[5 + BATCHES : 5 + 2 * BATCHES]
    wo_in = flights[5 + 2 * BATCHES]
    later = flights[6 + 2 * BATCHES :]
    scale = HEAD_DIM ** (-0.5)

    owner = lax.broadcasted_iota(jnp.int32, (many, width), 0) // heads
    which = lax.broadcasted_iota(jnp.int32, (many, width), 0) % heads
    own_head = lax.broadcasted_iota(jnp.int32, (many, width), 1) // HEAD_DIM == which
    for flight in flights[:4]:
        flight.wait()
    normed = rms_gain(x_v[...].astype(jnp.float32), gain_v[...][None]).astype(jnp.bfloat16)
    owner_slot = lax.broadcasted_iota(jnp.int32, (many, slots), 0) // heads
    filled = jnp.full((many, slots), len_s[0], jnp.int32)
    for r in range(1, rows):
        filled = jnp.where(owner_slot == r, len_s[r], filled)
    valid = lax.broadcasted_iota(jnp.int32, (many, slots), 1) < filled
    valid = valid & (spread(pad_v[...], owner_slot, rows) == 1)

    w_in.wait()
    def project(first, count):
        weight = w_v[pl.ds(first * width, count * width)]
        flat = rows_by_weight(normed, weight).astype(jnp.bfloat16).astype(jnp.float32)
        return [spread(flat[:, i * width : (i + 1) * width], owner, rows) for i in range(count)]

    query = jnp.where(own_head, project(0, 1)[0], 0.0)
    key_new, value_new = project(1, 2)
    own = jnp.sum(query * key_new, axis=1, keepdims=True) * scale
    scores = None
    for r in range(rows):
        if r % group == 0:
            k_in[r // group].wait()
        picked = jnp.where(owner == r, query, 0.0).astype(jnp.bfloat16)
        part = jnp.dot(picked, k_v[r], preferred_element_type=jnp.float32)
        scores = part if scores is None else scores + part
    scores = jnp.where(valid, scores * scale, NEG)
    top = jnp.maximum(jnp.max(scores, axis=1, keepdims=True), own)
    expo = jnp.exp(scores - top)
    own_exp = jnp.exp(own - top)
    inverse = 1.0 / (jnp.sum(expo, axis=1, keepdims=True) + own_exp)
    fresh = jnp.where(own_head, own_exp * inverse * value_new, 0.0)
    factor = jnp.where(own_head, inverse, 0.0)

    def fold(values):
        total = values
        for h in range(1, heads):
            total = total + pltpu.roll(values, many - h, 0)
        return jnp.concatenate([total[r * heads : r * heads + 1] for r in range(rows)], axis=0)

    fresh, factor = fold(fresh), fold(factor)

    lane = lax.broadcasted_iota(jnp.int32, (width, LANES), 1)
    columns = jnp.zeros((width, LANES), jnp.float32)
    for r in range(rows):
        if r % group == 0:
            v_in[r // group].wait()
        sums = []
        for h in range(heads):
            weights = expo[r * heads + h : r * heads + h + 1]
            acc = None
            for c in range(0, slots, LANES):
                block = v_v[r, pl.ds(h * HEAD_DIM, HEAD_DIM), pl.ds(c, LANES)].astype(jnp.float32)
                block = block * weights[:, c : c + LANES]
                acc = block if acc is None else acc + block
            sums.append(acc)
        column = jnp.sum(jnp.concatenate(sums, axis=0), axis=1, keepdims=True)
        columns = jnp.where(lane == r, column, columns)
    attn = (fresh + columns.T[:rows] * factor).astype(jnp.bfloat16)
    wo_in.wait()
    terms = jnp.dot(attn, wo_v[...], preferred_element_type=jnp.float32).astype(out_ref.dtype)
    for t in range(out_ref.shape[0]):
        out_ref[t] = terms
    for flight in later:
        flight.wait()


def mlp_kernel(parts_ref, x_ref, gain_ref, up_ref, down_ref, out_ref, resid_ref):
    resid = x_ref[...].astype(jnp.float32) + jnp.sum(parts_ref[...].astype(jnp.float32), axis=0)
    resid_ref[...] = resid
    inverse = lax.rsqrt(jnp.mean(resid * resid, axis=-1, keepdims=True) + 1e-06)
    scaled = (resid * gain_ref[...][None]).astype(jnp.bfloat16)
    hidden = jax.nn.gelu(rows_by_weight(scaled, up_ref[...]) * inverse, approximate=True)
    terms = jnp.dot(hidden.astype(jnp.bfloat16), down_ref[...], preferred_element_type=jnp.float32)
    terms = terms.astype(out_ref.dtype)
    for t in range(out_ref.shape[0]):
        out_ref[t] = terms


def head_kernel(parts_ref, resid_ref, head_ref, place_ref, out_ref, *, half):
    rows = resid_ref.shape[0]
    pairs = place_ref.shape[1]
    total = jnp.sum(parts_ref[...].astype(jnp.float32), axis=0)
    state = (resid_ref[...] + total).astype(jnp.bfloat16)
    head = rows_by_weight(state, head_ref[...])
    here = lax.axis_index("req")
    place = place_ref[...].astype(jnp.float32)
    wanted = jnp.where(here < half, place[0:1], place[1:2])
    eye = lax.broadcasted_iota(jnp.int32, (pairs, pairs), 0) == lax.broadcasted_iota(
        jnp.int32, (pairs, pairs), 1
    )
    column = jnp.sum(
        jnp.where(eye, jnp.broadcast_to(wanted, (pairs, pairs)), 0.0), axis=1, keepdims=True
    )
    base = ((here % half) * rows).astype(jnp.float32)
    picked = jnp.zeros((pairs, head.shape[1]), jnp.float32)
    for r in range(rows):
        picked = jnp.where(column == base + r, jnp.broadcast_to(head[r : r + 1], picked.shape), picked)
    out_ref[...] = picked.reshape(out_ref.shape)


def guide_kernel(arrived_ref, guide_ref, out_ref, value_v, sem, *, half):
    cond = jnp.sum(arrived_ref[:half], axis=0)
    uncond = jnp.sum(arrived_ref[half:], axis=0)
    weights = guide_ref[...][None]
    row = lax.broadcasted_iota(jnp.int32, cond.shape, 0)
    weight = jnp.broadcast_to(weights[:, 0:1], cond.shape)
    for j in range(1, cond.shape[0]):
        weight = jnp.where(row == j, jnp.broadcast_to(weights[:, j : j + 1], cond.shape), weight)
    value_v[...] = uncond + weight * (cond - uncond)
    copy = pltpu.make_async_copy(value_v, out_ref, sem)
    copy.start()
    copy.wait()


def whole(count, space):
    return [pl.BlockSpec(memory_space=space)] * count


def tp_exchange(parts):
    return lax.all_to_all(parts, "tp", 0, 0)


def on_device(
    inputs,
    gain_attn,
    w_qkv,
    k_cache,
    v_cache,
    lengths,
    pad_mask,
    w_out,
    gain_mlp,
    w_up,
    w_down,
    w_head,
    placement,
    guide,
):
    rows, model = inputs.shape
    width = w_qkv.shape[1]
    peers = lax.axis_size("tp")
    params = pltpu.CompilerParams(vmem_limit_bytes=VMEM_BYTES)
    parts_shape = jax.ShapeDtypeStruct((peers, rows, model), jnp.bfloat16)
    fused = w_qkv.reshape(-1, model)
    operands = (inputs, gain_attn, fused, k_cache, v_cache, lengths, pad_mask, w_out)
    operands += (w_up, w_down, w_head)
    kept = [jax.ShapeDtypeStruct(w.shape, w.dtype) for w in (w_up, w_down, w_head)]
    parts, w_up, w_down, w_head = pl.pallas_call(
        attend_kernel,
        out_shape=(parts_shape, *kept),
        in_specs=whole(11, pltpu.HBM),
        out_specs=tuple(whole(4, pltpu.VMEM)),
        scratch_shapes=[
            pltpu.VMEM(inputs.shape, inputs.dtype),
            pltpu.VMEM((model,), jnp.float32),
            pltpu.VMEM(fused.shape, fused.dtype),
            pltpu.VMEM(k_cache.shape, k_cache.dtype),
            pltpu.VMEM(v_cache.shape, v_cache.dtype),
            pltpu.SMEM(lengths.shape, lengths.dtype),
            pltpu.VMEM(pad_mask.shape, pad_mask.dtype),
            pltpu.VMEM(w_out.shape, w_out.dtype),
            pltpu.SemaphoreType.DMA((9 + 2 * BATCHES,)),
        ],
        compiler_params=params,
        name="attend",
    )(*(pltpu.with_memory_space_constraint(a, pltpu.HBM) for a in operands))
    parts, resid = pl.pallas_call(
        mlp_kernel,
        out_shape=(parts_shape, jax.ShapeDtypeStruct((rows, model), jnp.float32)),
        in_specs=whole(5, pltpu.VMEM),
        out_specs=tuple(whole(2, pltpu.VMEM)),
        compiler_params=params,
        name="mlp",
    )(tp_exchange(parts), inputs, gain_mlp, w_up, w_down)
    pairs_here = guide.shape[0]
    devices = lax.axis_size("req")
    slots = pl.pallas_call(
        functools.partial(head_kernel, half=devices // 2),
        out_shape=jax.ShapeDtypeStruct((devices, pairs_here, width), jnp.float32),
        in_specs=whole(4, pltpu.VMEM),
        out_specs=pl.BlockSpec(memory_space=pltpu.VMEM),
        compiler_params=params,
        name="head",
    )(tp_exchange(parts), resid, w_head, placement)
    arrived = lax.all_to_all(slots, "req", 0, 0)
    return pl.pallas_call(
        functools.partial(guide_kernel, half=devices // 2),
        out_shape=jax.ShapeDtypeStruct((pairs_here, width), jnp.float32),
        in_specs=whole(2, pltpu.VMEM),
        out_specs=pl.BlockSpec(memory_space=pltpu.HBM),
        scratch_shapes=[
            pltpu.VMEM((pairs_here, width), jnp.float32),
            pltpu.SemaphoreType.DMA(()),
        ],
        compiler_params=params,
        name="guide",
    )(arrived, guide)


def solution(mesh):
    placed = (
        P("req", None),
        P(),
        P(None, "tp", None),
        P("req", "tp", None),
        P("req", "tp", None),
        P("req"),
        P("req", None),
        P("tp", None),
        P(),
        P("tp", None),
        P("tp", None),
        P("tp", None),
        P(),
        P("req"),
    )
    return jax.shard_map(
        on_device, mesh=mesh, in_specs=placed, out_specs=P("req", "tp"), check_vma=False
    )
```

```python
import functools

import jax
import jax.numpy as jnp
from jax import lax
from jax.experimental import pallas as pl
from jax.experimental.pallas import tpu as pltpu
from jax.sharding import PartitionSpec as P

HEAD_DIM = 80
NEG = -1e30
LANES = 128
BATCHES = 2
VMEM_BYTES = 40 << 20


def rms_gain(values, gain):
    return values * lax.rsqrt(jnp.mean(values * values, axis=-1, keepdims=True) + 1e-06) * gain


def rows_by_weight(left, weight):
    return lax.dot_general(
        left, weight, (((1,), (1,)), ((), ())), preferred_element_type=jnp.float32
    )


def spread(values, owner, count):
    out = jnp.broadcast_to(values[0:1], owner.shape)
    for r in range(1, count):
        out = jnp.where(owner == r, jnp.broadcast_to(values[r : r + 1], owner.shape), out)
    return out


def attend_kernel(
    x_hbm,
    gain_hbm,
    w_hbm,
    k_hbm,
    v_hbm,
    len_hbm,
    pad_hbm,
    wo_hbm,
    out_ref,
    x_v,
    gain_v,
    w_v,
    k_v,
    v_v,
    len_s,
    pad_v,
    wo_v,
    sems,
):
    rows, width, slots = k_v.shape
    heads = width // HEAD_DIM
    many = rows * heads
    group = rows // BATCHES
    copies = [
        (x_hbm, x_v),
        (gain_hbm, gain_v),
        (len_hbm, len_s),
        (pad_hbm, pad_v),
        (w_hbm, w_v),
    ]
    for a, b in ((k_hbm, k_v), (v_hbm, v_v)):
        for i in range(BATCHES):
            part = pl.ds(i * group, group)
            copies.append((a.at[part], b.at[part]))
    copies.append((wo_hbm, wo_v))
    flights = [pltpu.make_async_copy(a, b, sems.at[i]) for i, (a, b) in enumerate(copies)]
    for i, flight in enumerate(flights):
        flight.start(priority=int(i >= 5 + BATCHES))
    w_in = flights[4]
    k_in = flights[5 : 5 + BATCHES]
    v_in = flights[5 + BATCHES : 5 + 2 * BATCHES]
    wo_in = flights[5 + 2 * BATCHES]
    scale = HEAD_DIM ** (-0.5)

    owner = lax.broadcasted_iota(jnp.int32, (many, width), 0) // heads
    which = lax.broadcasted_iota(jnp.int32, (many, width), 0) % heads
    own_head = lax.broadcasted_iota(jnp.int32, (many, width), 1) // HEAD_DIM == which
    for flight in flights[:4]:
        flight.wait()
    normed = rms_gain(x_v[...].astype(jnp.float32), gain_v[...][None]).astype(jnp.bfloat16)
    owner_slot = lax.broadcasted_iota(jnp.int32, (many, slots), 0) // heads
    filled = jnp.full((many, slots), len_s[0], jnp.int32)
    for r in range(1, rows):
        filled = jnp.where(owner_slot == r, len_s[r], filled)
    valid = lax.broadcasted_iota(jnp.int32, (many, slots), 1) < filled
    valid = valid & (spread(pad_v[...], owner_slot, rows) == 1)

    w_in.wait()
    def project(first, count):
        weight = w_v[pl.ds(first * width, count * width)]
        flat = rows_by_weight(normed, weight).astype(jnp.bfloat16).astype(jnp.float32)
        return [spread(flat[:, i * width : (i + 1) * width], owner, rows) for i in range(count)]

    query = jnp.where(own_head, project(0, 1)[0], 0.0)
    key_new, value_new = project(1, 2)
    own = jnp.sum(query * key_new, axis=1, keepdims=True) * scale
    scores = None
    for r in range(rows):
        if r % group == 0:
            k_in[r // group].wait()
        picked = jnp.where(owner == r, query, 0.0).astype(jnp.bfloat16)
        part = jnp.dot(picked, k_v[r], preferred_element_type=jnp.float32)
        scores = part if scores is None else scores + part
    scores = jnp.where(valid, scores * scale, NEG)
    top = jnp.maximum(jnp.max(scores, axis=1, keepdims=True), own)
    expo = jnp.exp(scores - top)
    own_exp = jnp.exp(own - top)
    inverse = 1.0 / (jnp.sum(expo, axis=1, keepdims=True) + own_exp)
    probs = (expo * inverse).astype(jnp.bfloat16).astype(jnp.float32)
    own_prob = (own_exp * inverse).astype(jnp.bfloat16).astype(jnp.float32)
    fresh = jnp.where(own_head, own_prob * value_new, 0.0)
    mixed = fresh
    for h in range(1, heads):
        mixed = mixed + pltpu.roll(fresh, many - h, 0)
    mixed = jnp.concatenate([mixed[r * heads : r * heads + 1] for r in range(rows)], axis=0)

    lane = lax.broadcasted_iota(jnp.int32, (width, LANES), 1)
    columns = jnp.zeros((width, LANES), jnp.float32)
    for r in range(rows):
        if r % group == 0:
            v_in[r // group].wait()
        sums = []
        for h in range(heads):
            weights = probs[r * heads + h : r * heads + h + 1]
            acc = None
            for c in range(0, slots, LANES):
                block = v_v[r, pl.ds(h * HEAD_DIM, HEAD_DIM), pl.ds(c, LANES)].astype(jnp.float32)
                block = block * weights[:, c : c + LANES]
                acc = block if acc is None else acc + block
            sums.append(acc)
        column = jnp.sum(jnp.concatenate(sums, axis=0), axis=1, keepdims=True)
        columns = jnp.where(lane == r, column, columns)
    attn = (mixed + columns.T[:rows]).astype(jnp.bfloat16)
    wo_in.wait()
    terms = jnp.dot(attn, wo_v[...], preferred_element_type=jnp.float32).astype(out_ref.dtype)
    for t in range(out_ref.shape[0]):
        out_ref[t] = terms


def mlp_kernel(parts_ref, x_ref, gain_ref, up_ref, down_ref, out_ref, resid_ref):
    resid = x_ref[...].astype(jnp.float32) + jnp.sum(parts_ref[...].astype(jnp.float32), axis=0)
    resid_ref[...] = resid
    inverse = lax.rsqrt(jnp.mean(resid * resid, axis=-1, keepdims=True) + 1e-06)
    scaled = (resid * gain_ref[...][None]).astype(jnp.bfloat16)
    hidden = jax.nn.gelu(rows_by_weight(scaled, up_ref[...]) * inverse, approximate=True)
    terms = jnp.dot(hidden.astype(jnp.bfloat16), down_ref[...], preferred_element_type=jnp.float32)
    terms = terms.astype(out_ref.dtype)
    for t in range(out_ref.shape[0]):
        out_ref[t] = terms


def head_kernel(parts_ref, resid_ref, head_ref, place_ref, out_ref, *, half):
    rows = resid_ref.shape[0]
    pairs = place_ref.shape[1]
    total = jnp.sum(parts_ref[...].astype(jnp.float32), axis=0)
    state = (resid_ref[...] + total).astype(jnp.bfloat16)
    head = rows_by_weight(state, head_ref[...])
    here = lax.axis_index("req")
    place = place_ref[...].astype(jnp.float32)
    wanted = jnp.where(here < half, place[0:1], place[1:2])
    eye = lax.broadcasted_iota(jnp.int32, (pairs, pairs), 0) == lax.broadcasted_iota(
        jnp.int32, (pairs, pairs), 1
    )
    column = jnp.sum(
        jnp.where(eye, jnp.broadcast_to(wanted, (pairs, pairs)), 0.0), axis=1, keepdims=True
    )
    base = ((here % half) * rows).astype(jnp.float32)
    picked = jnp.zeros((pairs, head.shape[1]), jnp.float32)
    for r in range(rows):
        picked = jnp.where(column == base + r, jnp.broadcast_to(head[r : r + 1], picked.shape), picked)
    out_ref[...] = picked.reshape(out_ref.shape)


def guide_kernel(arrived_ref, guide_ref, out_ref, value_v, sem, *, half):
    cond = jnp.sum(arrived_ref[:half], axis=0)
    uncond = jnp.sum(arrived_ref[half:], axis=0)
    weights = guide_ref[...][None]
    row = lax.broadcasted_iota(jnp.int32, cond.shape, 0)
    weight = jnp.broadcast_to(weights[:, 0:1], cond.shape)
    for j in range(1, cond.shape[0]):
        weight = jnp.where(row == j, jnp.broadcast_to(weights[:, j : j + 1], cond.shape), weight)
    value_v[...] = uncond + weight * (cond - uncond)
    copy = pltpu.make_async_copy(value_v, out_ref, sem)
    copy.start()
    copy.wait()


def whole(count, space):
    return [pl.BlockSpec(memory_space=space)] * count


def tp_exchange(parts):
    return lax.all_to_all(parts, "tp", 0, 0)


def on_device(
    inputs,
    gain_attn,
    w_qkv,
    k_cache,
    v_cache,
    lengths,
    pad_mask,
    w_out,
    gain_mlp,
    w_up,
    w_down,
    w_head,
    placement,
    guide,
):
    rows, model = inputs.shape
    width = w_qkv.shape[1]
    peers = lax.axis_size("tp")
    params = pltpu.CompilerParams(vmem_limit_bytes=VMEM_BYTES)
    parts_shape = jax.ShapeDtypeStruct((peers, rows, model), jnp.bfloat16)
    fused = w_qkv.reshape(-1, model)
    operands = (inputs, gain_attn, fused, k_cache, v_cache, lengths, pad_mask, w_out)
    parts = pl.pallas_call(
        attend_kernel,
        out_shape=parts_shape,
        in_specs=whole(8, pltpu.HBM),
        out_specs=pl.BlockSpec(memory_space=pltpu.VMEM),
        scratch_shapes=[
            pltpu.VMEM(inputs.shape, inputs.dtype),
            pltpu.VMEM((model,), jnp.float32),
            pltpu.VMEM(fused.shape, fused.dtype),
            pltpu.VMEM(k_cache.shape, k_cache.dtype),
            pltpu.VMEM(v_cache.shape, v_cache.dtype),
            pltpu.SMEM(lengths.shape, lengths.dtype),
            pltpu.VMEM(pad_mask.shape, pad_mask.dtype),
            pltpu.VMEM(w_out.shape, w_out.dtype),
            pltpu.SemaphoreType.DMA((6 + 2 * BATCHES,)),
        ],
        compiler_params=params,
        name="attend",
    )(*(pltpu.with_memory_space_constraint(a, pltpu.HBM) for a in operands))
    parts, resid = pl.pallas_call(
        mlp_kernel,
        out_shape=(parts_shape, jax.ShapeDtypeStruct((rows, model), jnp.float32)),
        in_specs=whole(5, pltpu.VMEM),
        out_specs=tuple(whole(2, pltpu.VMEM)),
        compiler_params=params,
        name="mlp",
    )(tp_exchange(parts), inputs, gain_mlp, w_up, w_down)
    pairs_here = guide.shape[0]
    devices = lax.axis_size("req")
    slots = pl.pallas_call(
        functools.partial(head_kernel, half=devices // 2),
        out_shape=jax.ShapeDtypeStruct((devices, pairs_here, width), jnp.float32),
        in_specs=whole(4, pltpu.VMEM),
        out_specs=pl.BlockSpec(memory_space=pltpu.VMEM),
        compiler_params=params,
        name="head",
    )(tp_exchange(parts), resid, w_head, placement)
    arrived = lax.all_to_all(slots, "req", 0, 0)
    return pl.pallas_call(
        functools.partial(guide_kernel, half=devices // 2),
        out_shape=jax.ShapeDtypeStruct((pairs_here, width), jnp.float32),
        in_specs=whole(2, pltpu.VMEM),
        out_specs=pl.BlockSpec(memory_space=pltpu.HBM),
        scratch_shapes=[
            pltpu.VMEM((pairs_here, width), jnp.float32),
            pltpu.SemaphoreType.DMA(()),
        ],
        compiler_params=params,
        name="guide",
    )(arrived, guide)


def solution(mesh):
    placed = (
        P("req", None),
        P(),
        P(None, "tp", None),
        P("req", "tp", None),
        P("req", "tp", None),
        P("req"),
        P("req", None),
        P("tp", None),
        P(),
        P("tp", None),
        P("tp", None),
        P("tp", None),
        P(),
        P("req"),
    )
    return jax.shard_map(
        on_device, mesh=mesh, in_specs=placed, out_specs=P("req", "tp"), check_vma=False
    )
```
